32 devices in a mesh: row: 4 (over z), col: 8 (over y, x, core).
Axes of the slice: x: 2, y: 2, z: 4, core: 2. Of those that a mesh axis runs over, the one named last changes fastest.
Arguments:
- resident: float32 [1536, 1536], P('row', 'col'), may hold values from -6 to 6
- factor_one: float32 [1536, 512], P(('row', 'col')), may hold values from -0.15625 to 0.15625
- pattern_one: int32 [96], P(('row', 'col')), may hold values 0 or 1
- factor_two: float32 [1536, 512], P(('row', 'col')), may hold values from -0.15625 to 0.15625
- pattern_two: int32 [96], P(('row', 'col')), may hold values 0 or 1
- coupling: float32 [512, 512], replicated, may hold values from -0.25 to 0.25
- diagonal_one: float32 [512, 512], replicated, may hold values from -6 to 6
- diagonal_two: float32 [512, 512], replicated, may hold values from -6 to 6
Outputs:
- inverse_one: float32 [1536, 512], P(('row', 'col'))
- block_one: float32 [512, 512], replicated
- inverse_two: float32 [1536, 512], P(('row', 'col'))
- coupled: float32 [512, 512], replicated
- block_two: float32 [512, 512], replicated
The draws below stay inside these ranges and needn't reach their ends.
Inputs may be any that keep to these rules, and one draw needn't show every extreme that they name: `pattern_one`: 1 keeps a block of 16 factor rows, 0 marks it structurally zero. `pattern_two`: 1 keeps a block of 16 factor rows, 0 marks it structurally zero.
All inputs are finite; a program needn't handle non-finite values.
Results may differ from the reference program's by a relative error of at most 0.00007.
Values sent between devices are 32-bit elements; how exact they have to be, the bound alone decides.
No kernel may reach another device: no remote copies, remote signals or barrier semaphores. Data moves between devices by JAX's collectives and lax.ppermute only.
A program may use at most 64 MiB of HBM per device.

```python
import jax
import jax.numpy as jnp
from jax import lax

W = 512
ORDER = 1536
NBLK = 96


def set_ends(entries, own_key, low, largest):
    index_at = [jax.random.randint(jax.random.fold_in(own_key, axis), (), 0, length) for axis, length in enumerate(entries.shape)]
    widest = entries.shape.index(max(entries.shape))
    beside = index_at[:widest] + [(index_at[widest] + 1) % entries.shape[widest]] + index_at[widest + 1:]
    return entries.at[tuple(index_at)].set(low).at[tuple(beside)].set(largest)


def shard_levels(key, extent, split, least, top_value):
    level = 1.0
    for axis_at, blocks in split:
        steps = jax.random.uniform(jax.random.fold_in(jax.random.fold_in(key, 6), axis_at), (blocks,), jnp.float32, least / len(split), top_value / len(split))
        level = level * jnp.repeat(jnp.exp(steps), extent[axis_at] // blocks).reshape((-1,) + (1,) * (len(extent) - 1 - axis_at))
    return level


def scatter_about(stream_key, dims, spread, limit, shards=(), dtype=jnp.bfloat16):
    entries = jax.random.normal(stream_key, dims, jnp.float32) * spread
    if len(shards) > 0:
        entries = shard_levels(stream_key, dims, shards, -0.22, 0.18) * entries
    return jnp.clip(entries, min=-limit, max=limit).astype(dtype)


def setup_inputs(seed: int = 0) -> dict:
    splits = jax.random.split(jax.random.key(seed), 9)
    return {
        "resident": scatter_about(splits[0], (ORDER, ORDER), 1.0, 6.0, ((0, 4), (1, 8)), jnp.float32),
        "factor_one": scatter_about(splits[1], (ORDER, W), ORDER ** -0.5, 0.15625, ((0, 32),), jnp.float32),
        "pattern_one": set_ends((jax.random.randint(splits[2], (NBLK,), 0, 4) < 3).astype(jnp.int32), jax.random.fold_in(splits[2], 1), 0, 1),
        "factor_two": scatter_about(splits[3], (ORDER, W), ORDER ** -0.5, 0.15625, ((0, 32),), jnp.float32),
        "pattern_two": set_ends((jax.random.randint(splits[4], (NBLK,), 0, 4) < 3).astype(jnp.int32), jax.random.fold_in(splits[4], 1), 0, 1),
        "coupling": scatter_about(splits[5], (W, W), W ** -0.5, 0.25, (), jnp.float32),
        "diagonal_one": scatter_about(splits[6], (W, W), 1.0, 6.0, (), jnp.float32),
        "diagonal_two": scatter_about(splits[7], (W, W), 1.0, 6.0, (), jnp.float32),
    }


def masked(factor, pattern):
    block_count = pattern.shape[0]
    row_count, col_width = factor.shape
    shaped = factor.reshape(block_count, row_count // block_count, col_width)
    return (shaped * pattern.astype(jnp.float32)[:, None, None]).reshape(row_count, col_width)


def reference(resident, factor_one, pattern_one, factor_two, pattern_two, coupling, diagonal_one, diagonal_two):
    high = lax.Precision.HIGHEST
    first = masked(factor_one, pattern_one)
    second = masked(factor_two, pattern_two)
    inverse_one = -jnp.dot(resident, first, precision=high, preferred_element_type=jnp.float32)
    block_one = diagonal_one - jnp.einsum("ka,kb->ab", first, inverse_one, precision=high)
    coupled = -(jnp.einsum("ka,kb->ab", inverse_one, second, precision=high) + jnp.dot(block_one, coupling, precision=high))
    inverse_two = -(jnp.dot(resident, second, precision=high, preferred_element_type=jnp.float32) + jnp.dot(inverse_one, coupling, precision=high))
    block_two = diagonal_two - jnp.einsum("ka,kb->ab", second, inverse_two, precision=high) - jnp.einsum("ka,kb->ab", coupling, coupled, precision=high)
    return (inverse_one, block_one, inverse_two, coupled, block_two)
```

```python
import jax
import jax.numpy as jnp
from jax import lax
from jax.sharding import PartitionSpec as P

HIGH = lax.Precision.HIGHEST


def masked(factor, pattern):
    block_count = pattern.shape[0]
    row_count, col_width = factor.shape
    shaped = factor.reshape(block_count, row_count // block_count, col_width)
    return (shaped * pattern.astype(jnp.float32)[:, None, None]).reshape(row_count, col_width)


def tdot(left, right):
    return lax.dot_general(
        left,
        right,
        (((0,), (0,)), ((), ())),
        precision=HIGH,
        preferred_element_type=jnp.float32,
    )


def cut(value, start, length, axis):
    return lax.dynamic_slice_in_dim(value, start, length, axis)


def put(whole, piece, *start):
    lead = len(start)
    shaped = piece.reshape((1,) * lead + piece.shape)
    return lax.dynamic_update_slice(whole, shaped, (*start, *(0,) * piece.ndim))


def row_xor(value, bit):
    count = lax.axis_size("row")
    return lax.ppermute(value, "row", [(at, at ^ bit) for at in range(count)])


def col_xor(value, bits):
    count = lax.axis_size("col")
    return lax.ppermute(value, "col", [(at, at ^ bits) for at in range(count)])


def body(
    resident, factor_one, pattern_one, factor_two, pattern_two, coupling, diagonal_one, diagonal_two
):
    planes, columns = lax.axis_size("row"), lax.axis_size("col")
    ratio, chips = columns // planes, columns // 2
    plane, column = lax.axis_index("row"), lax.axis_index("col")
    core, chip = column % 2, column // 2
    block, width = factor_one.shape
    rows = resident.shape[0]
    piece = width // chips

    first = masked(factor_one, pattern_one)
    second = masked(factor_two, pattern_two)
    joined = second - jnp.dot(first, coupling, precision=HIGH)

    own = jnp.concatenate([first, joined], 1)
    strip = [own] + [
        lax.ppermute(own, "row", [(at, (at + step) % planes) for at in range(planes)])
        for step in range(1, planes)
    ]
    strip = jnp.concatenate(strip, 0)

    turned = resident.T
    arrived = []
    for step in range(planes):
        part = cut(turned, (step + column // ratio) % planes * block, block, 0)
        route = [(at, planes * (at % ratio) + (step + at // ratio) % planes) for at in range(columns)]
        arrived.append(lax.ppermute(part, "col", route))
    arrived = jnp.concatenate(arrived + arrived, 0)
    tile = cut(arrived, (column % planes - plane) % planes * block, planes * block, 0)

    plain = jnp.concatenate([first, second], 1)
    gathered = jnp.zeros((chips, 2, block, 2 * width), jnp.float32)
    for step in range(chips):
        moved = plain if step == 0 else col_xor(plain, 2 * step)
        gathered = put(gathered, moved, chip ^ step, core)
    mine = lax.dynamic_slice_in_dim(gathered, core, 1, 1)
    gathered = lax.dynamic_update_slice(gathered, col_xor(mine, 1), (0, 1 - core, 0, 0))
    factors = gathered.reshape(rows, 2 * width)

    given = col_xor(tdot(tile, cut(strip, (1 - core) * width, width, 1)), 1)
    half = tdot(tile, cut(strip, core * width, width, 1)) + given
    product = cut(half, chip * piece, piece, 1)
    for step in range(1, chips):
        product += col_xor(cut(half, (chip ^ step) * piece, piece, 1), 2 * step)

    partner = col_xor(product, 1)
    leading = jnp.where(core == 0, product, partner)
    square = tdot(cut(factors, core * width, width, 1), product)
    part = width // 2
    crossed = tdot(leading, cut(factors, width + core * part, part, 1))
    crossed = crossed.reshape(piece, part // piece, piece).transpose(1, 0, 2).reshape(part, piece)
    total = jnp.concatenate([square, crossed], 0)

    middle = total.shape[0] // 2
    odd = plane % 2
    kept = cut(total, odd * middle, middle, 0) + row_xor(cut(total, (1 - odd) * middle, middle, 0), 1)
    bit = 2
    while bit < planes:
        kept += row_xor(kept, bit)
        bit *= 2
    other = row_xor(kept, 1)

    everything = jnp.zeros((2, chips, 2, middle, piece), jnp.float32)
    for source, at in ((kept, odd), (other, 1 - odd)):
        for step in range(chips):
            moved = source if step == 0 else col_xor(source, 2 * step)
            everything = put(everything, moved, core, chip ^ step, at)
    mine = lax.dynamic_slice_in_dim(everything, core, 1, 0)
    everything = lax.dynamic_update_slice(everything, col_xor(mine, 1), (1 - core, 0, 0, 0, 0))
    everything = everything.reshape(2, chips, 2 * middle, piece)

    sheet = product.reshape(columns, block, piece)
    sheet = lax.all_to_all(sheet, "col", 0, 0)
    sheet = sheet.reshape(chips, 2, block, piece).transpose(1, 2, 0, 3).reshape(2, block, width)
    inverse_one, inverse_two = -sheet[0], -sheet[1]

    squares = everything[:, :, :width].transpose(0, 2, 1, 3).reshape(2, width, width)
    cross = everything[:, :, width:].reshape(2, chips, part // piece, piece, piece)
    cross = cross.transpose(1, 3, 0, 2, 4).reshape(width, width)
    block_one = diagonal_one + squares[0]
    coupled = cross - jnp.dot(block_one, coupling, precision=HIGH)
    block_two = diagonal_two + squares[1] - tdot(coupling, coupled)
    return (inverse_one, block_one, inverse_two, coupled, block_two)


def solution(mesh):
    return jax.shard_map(
        body,
        mesh=mesh,
        in_specs=(
            P("row", "col"),
            P(("row", "col"), None),
            P(("row", "col")),
            P(("row", "col"), None),
            P(("row", "col")),
            P(),
            P(),
            P(),
        ),
        out_specs=(P(("row", "col"), None), P(), P(("row", "col"), None), P(), P()),
        check_vma=False,
    )
```

```python
import functools

import jax
import jax.numpy as jnp
from jax import lax
from jax.experimental import pallas as pl
from jax.experimental.pallas import tpu as pltpu
from jax.sharding import PartitionSpec as P

HIGH = lax.Precision.HIGHEST


def masked(factor, pattern):
    block_count = pattern.shape[0]
    row_count, col_width = factor.shape
    shaped = factor.reshape(block_count, row_count // block_count, col_width)
    return (shaped * pattern.astype(jnp.float32)[:, None, None]).reshape(row_count, col_width)


def tdot(left, right):
    return lax.dot_general(
        left,
        right,
        (((0,), (0,)), ((), ())),
        precision=HIGH,
        preferred_element_type=jnp.float32,
    )


def cut(value, start, length, axis):
    return lax.dynamic_slice_in_dim(value, start, length, axis)


def put(whole, piece, *start):
    lead = len(start)
    shaped = piece.reshape((1,) * lead + piece.shape)
    return lax.dynamic_update_slice(whole, shaped, (*start, *(0,) * piece.ndim))


def row_xor(value, bit):
    count = lax.axis_size("row")
    return lax.ppermute(value, "row", [(at, at ^ bit) for at in range(count)])


def col_xor(value, bits):
    count = lax.axis_size("col")
    return lax.ppermute(value, "col", [(at, at ^ bits) for at in range(count)])


def narrow_body(
    resident, factor_one, pattern_one, factor_two, pattern_two, coupling, diagonal_one, diagonal_two
):
    planes, columns = lax.axis_size("row"), lax.axis_size("col")
    ratio, chips = columns // planes, columns // 2
    plane, column = lax.axis_index("row"), lax.axis_index("col")
    core, chip = column % 2, column // 2
    block, width = factor_one.shape
    rows = resident.shape[0]
    piece = width // chips

    first = masked(factor_one, pattern_one)
    second = masked(factor_two, pattern_two)
    joined = second - jnp.dot(first, coupling, precision=HIGH)

    own = jnp.concatenate([first, joined], 1)
    strip = [own] + [
        lax.ppermute(own, "row", [(at, (at + step) % planes) for at in range(planes)])
        for step in range(1, planes)
    ]
    strip = jnp.concatenate(strip, 0)

    turned = resident.T
    arrived = []
    for step in range(planes):
        part = cut(turned, (step + column // ratio) % planes * block, block, 0)
        route = [(at, planes * (at % ratio) + (step + at // ratio) % planes) for at in range(columns)]
        arrived.append(lax.ppermute(part, "col", route))
    arrived = jnp.concatenate(arrived + arrived, 0)
    tile = cut(arrived, (column % planes - plane) % planes * block, planes * block, 0)

    plain = jnp.concatenate([first, second], 1)
    gathered = jnp.zeros((chips, 2, block, 2 * width), jnp.float32)
    for step in range(chips):
        moved = plain if step == 0 else col_xor(plain, 2 * step)
        gathered = put(gathered, moved, chip ^ step, core)
    mine = lax.dynamic_slice_in_dim(gathered, core, 1, 1)
    gathered = lax.dynamic_update_slice(gathered, col_xor(mine, 1), (0, 1 - core, 0, 0))
    factors = gathered.reshape(rows, 2 * width)

    given = col_xor(tdot(tile, cut(strip, (1 - core) * width, width, 1)), 1)
    half = tdot(tile, cut(strip, core * width, width, 1)) + given
    product = cut(half, chip * piece, piece, 1)
    for step in range(1, chips):
        product += col_xor(cut(half, (chip ^ step) * piece, piece, 1), 2 * step)

    partner = col_xor(product, 1)
    leading = jnp.where(core == 0, product, partner)
    square = tdot(cut(factors, core * width, width, 1), product)
    part = width // 2
    crossed = tdot(leading, cut(factors, width + core * part, part, 1))
    crossed = crossed.reshape(piece, part // piece, piece).transpose(1, 0, 2).reshape(part, piece)
    total = jnp.concatenate([square, crossed], 0)

    middle = total.shape[0] // 2
    odd = plane % 2
    kept = cut(total, odd * middle, middle, 0) + row_xor(cut(total, (1 - odd) * middle, middle, 0), 1)
    bit = 2
    while bit < planes:
        kept += row_xor(kept, bit)
        bit *= 2
    other = row_xor(kept, 1)

    everything = jnp.zeros((2, chips, 2, middle, piece), jnp.float32)
    for source, at in ((kept, odd), (other, 1 - odd)):
        for step in range(chips):
            moved = source if step == 0 else col_xor(source, 2 * step)
            everything = put(everything, moved, core, chip ^ step, at)
    mine = lax.dynamic_slice_in_dim(everything, core, 1, 0)
    everything = lax.dynamic_update_slice(everything, col_xor(mine, 1), (1 - core, 0, 0, 0, 0))
    everything = everything.reshape(2, chips, 2 * middle, piece)

    sheet = product.reshape(columns, block, piece)
    sheet = lax.all_to_all(sheet, "col", 0, 0)
    sheet = sheet.reshape(chips, 2, block, piece).transpose(1, 2, 0, 3).reshape(2, block, width)
    inverse_one, inverse_two = -sheet[0], -sheet[1]

    squares = everything[:, :, :width].transpose(0, 2, 1, 3).reshape(2, width, width)
    cross = everything[:, :, width:].reshape(2, chips, part // piece, piece, piece)
    cross = cross.transpose(1, 3, 0, 2, 4).reshape(width, width)
    block_one = diagonal_one + squares[0]
    coupled = cross - jnp.dot(block_one, coupling, precision=HIGH)
    block_two = diagonal_two + squares[1] - tdot(coupling, coupled)
    return (inverse_one, block_one, inverse_two, coupled, block_two)


def split(value):
    top = value.astype(jnp.bfloat16)
    return top, (value - top.astype(jnp.float32)).astype(jnp.bfloat16)


def fine_dot(left, right):
    def one(a, b):
        return jnp.dot(a, b, preferred_element_type=jnp.float32)

    return one(left[0], right[1]) + one(left[1], right[0]) + one(left[0], right[0])


def call(kernel, outs, *args, scalars=0, flops=0, scratch=()):
    outs = [jax.ShapeDtypeStruct(shape, kind) for shape, kind in outs]
    moved = sum(a.size * a.dtype.itemsize for a in (*args, *outs))
    return pl.pallas_call(
        kernel,
        out_shape=outs,
        in_specs=[pl.BlockSpec(memory_space=pltpu.SMEM)] * scalars
        + [pl.BlockSpec(memory_space=pltpu.VMEM)] * (len(args) - scalars),
        out_specs=[pl.BlockSpec(memory_space=pltpu.VMEM)] * len(outs),
        scratch_shapes=[pltpu.VMEM(shape, jnp.float32) for shape in scratch],
        cost_estimate=pl.CostEstimate(flops=flops, bytes_accessed=moved, transcendentals=0),
        compiler_params=pltpu.CompilerParams(vmem_limit_bytes=24 << 20),
    )(*args)


def span(start, length, step):
    return pl.ds(pl.multiple_of(start, step), length)


def place():
    plane, column = lax.axis_index("row"), lax.axis_index("col")
    return plane, column, column % 2, column // 2


def front_kernel(planes, ratio, one, two, f_one, f_two, coupling, turned, own, plain, *parts):
    column = place()[1]
    block, width = f_one.shape
    count = one.shape[0]
    tall = block // count
    for step, part in enumerate(parts):
        start = (step + column // ratio) % planes * block
        part[...] = turned[span(start, block, 8), :]
    for at in range(count):
        rows = slice(at * tall, (at + 1) * tall)
        first = f_one[rows, :] * one[at].astype(jnp.float32)
        plain[rows, :width] = first
        own[rows, :width] = first
        plain[rows, width:] = f_two[rows, :] * two[at].astype(jnp.float32)
    product = fine_dot(split(plain[:, :width]), split(coupling[...]))
    own[:, width:] = plain[:, width:] - product


def coupling_kernel(coupling, top, low, turned_top, turned_low):
    top[...], low[...] = split(coupling[...])
    turned_top[...], turned_low[...] = split(coupling[...].T)


def tile_kernel(planes, *refs):
    arrived, (top, low, held) = refs[:planes], refs[planes:]
    plane, column = place()[:2]
    block = arrived[0].shape[0]
    for step, part in enumerate(arrived):
        slot = (column + planes - step) % planes ^ plane
        held[span(slot * block, block, 8), :] = part[...]
    top[...], low[...] = split(held[...].T)


def part_kernel(away, top, low, *refs):
    strip, out = refs[:-1], refs[-1]
    width = out.shape[1]
    core = place()[2]
    side = 1 - core if away else core
    right = jnp.concatenate([part[:, span(side * width, width, 128)] for part in strip], 0)
    out[...] = fine_dot((top[...], low[...]), split(right))


def share_kernel(half, given, *outs):
    chip = place()[3]
    piece = outs[0].shape[1]
    for step, out in enumerate(outs):
        lanes = span((chip ^ step) * piece, piece, 128)
        out[...] = half[:, lanes] + given[:, lanes]


def sum_kernel(*refs):
    total = refs[0][...]
    for ref in refs[1:-1]:
        total += ref[...]
    refs[-1][...] = total


def factor_kernel(chips, *refs):
    parts, (top, low, held) = refs[: 2 * chips], refs[2 * chips :]
    core, chip = place()[2:]
    block = parts[0].shape[0]
    width = held.shape[1] // 2
    for at, part in enumerate(parts):
        row = (chip ^ at // 2) * 2 + (core ^ at % 2)
        held[span(row * block, block, 8), :] = part[...]
    top[:width], low[:width] = split(held[:, span(core * width, width, 128)].T)
    rest = width // 2
    top[width:], low[width:] = split(held[:, span(width + core * rest, rest, 128)].T)


def square_kernel(top, low, product, out):
    width = out.shape[0]
    out[...] = fine_dot((top[:width], low[:width]), split(product[...]))


def cross_kernel(top, low, product, partner, square, kept, sent, held):
    plane, _, core, _ = place()
    width, piece = square.shape
    leading = jnp.where(core == 0, product[...], partner[...])
    crossed = fine_dot((top[width:], low[width:]), split(leading))
    held[:width, :] = square[...]
    for start in range(0, width // 2, piece):
        held[width + start : width + start + piece, :] = crossed[start : start + piece].T
    middle = kept.shape[0]
    kept[...] = held[span(plane % 2 * middle, middle, 8), :]
    sent[...] = held[span((1 - plane % 2) * middle, middle, 8), :]


def last_kernel(chips, c_top, c_low, t_top, t_low, d_one, d_two, *refs):
    parts, (b_one, coupled, b_two, held) = refs[: 4 * chips], refs[4 * chips :]
    plane, _, core, chip = place()
    middle, piece = parts[0].shape
    width = b_one.shape[0]
    for at, part in enumerate(parts):
        side, step, half = core ^ at % 2, at // 2 % chips, plane % 2 ^ at // (2 * chips)
        held[side * chips + (chip ^ step), span(half * middle, middle, 8), :] = part[...]
    rest = width // 2
    for at in range(chips):
        lanes = slice(at * piece, (at + 1) * piece)
        b_one[:, lanes] = d_one[:, lanes] + held[at, :width, :]
        for start in range(0, width, piece):
            row = width + start % rest
            coupled[lanes, start : start + piece] = held[
                start // rest * chips + at, row : row + piece, :
            ]
    coupled[...] -= fine_dot(split(b_one[...]), (c_top[...], c_low[...]))
    again = fine_dot((t_top[...], t_low[...]), split(coupled[...]))
    for at in range(chips):
        lanes = slice(at * piece, (at + 1) * piece)
        b_two[:, lanes] = d_two[:, lanes] + held[chips + at, :width, :] - again[:, lanes]


def body(
    resident, factor_one, pattern_one, factor_two, pattern_two, coupling, diagonal_one, diagonal_two
):
    planes, columns = lax.axis_size("row"), lax.axis_size("col")
    ratio, chips = columns // planes, columns // 2
    block, width = factor_one.shape
    rows = resident.shape[0]
    piece = width // chips
    if piece % 128:
        return narrow_body(
            resident, factor_one, pattern_one, factor_two, pattern_two, coupling, diagonal_one, diagonal_two
        )
    f32, b16 = jnp.float32, jnp.bfloat16

    own, plain, *parts = call(
        functools.partial(front_kernel, planes, ratio),
        [((block, 2 * width), f32)] * 2 + [((block, rows), f32)] * planes,
        pattern_one,
        pattern_two,
        factor_one,
        factor_two,
        coupling,
        resident.T,
        scalars=2,
    )
    strip = [own]
    bit = 1
    while bit < planes:
        strip += [row_xor(value, bit) for value in strip]
        bit *= 2
    arrived = []
    for step, part in enumerate(parts):
        route = [(at, planes * (at % ratio) + (step + at // ratio) % planes) for at in range(columns)]
        arrived.append(lax.ppermute(part, "col", route))
    around = [plain] + [col_xor(plain, 2 * step) for step in range(1, chips)]
    factors = []
    for value in around:
        factors += [value, col_xor(value, 1)]

    c_split = call(coupling_kernel, [((width, width), b16)] * 4, coupling)
    tile = call(
        functools.partial(tile_kernel, planes),
        [((rows, planes * block), b16)] * 2,
        *arrived,
        scratch=[(planes * block, rows)],
    )

    work = 6 * rows * planes * block * width
    (away,) = call(functools.partial(part_kernel, True), [((rows, width), f32)], *tile, *strip, flops=work)
    (half,) = call(functools.partial(part_kernel, False), [((rows, width), f32)], *tile, *strip, flops=work)
    shares = call(share_kernel, [((rows, piece), f32)] * chips, half, col_xor(away, 1))
    shares = [shares[0]] + [col_xor(shares[step], 2 * step) for step in range(1, chips)]
    (product,) = call(sum_kernel, [((rows, piece), f32)], *shares)

    part = width // 2
    turned = call(
        functools.partial(factor_kernel, chips),
        [((width + part, rows), b16)] * 2,
        *factors,
        scratch=[(rows, 2 * width)],
    )
    (square,) = call(square_kernel, [((width, piece), f32)], *turned, product, flops=6 * width * rows * piece)
    middle = (width + part) // 2
    kept, sent = call(
        cross_kernel,
        [((middle, piece), f32)] * 2,
        *turned,
        product,
        col_xor(product, 1),
        square,
        flops=3 * width * rows * piece,
        scratch=[(width + part, piece)],
    )

    kept += row_xor(sent, 1)
    bit = 2
    while bit < planes:
        kept += row_xor(kept, bit)
        bit *= 2
    sheet = lax.all_to_all(product.reshape(columns, block, piece), "col", 0, 0)
    kept, sheet = lax.optimization_barrier((kept, sheet))
    sheet = sheet.reshape(chips, 2, block, piece).transpose(1, 2, 0, 3).reshape(2, block, width)
    inverse_one, inverse_two = -sheet[0], -sheet[1]

    everything = []
    for source in (kept, row_xor(kept, 1)):
        for step in range(chips):
            moved = source if step == 0 else col_xor(source, 2 * step)
            everything += [moved, col_xor(moved, 1)]
    block_one, coupled, block_two = call(
        functools.partial(last_kernel, chips),
        [((width, width), f32)] * 3,
        *c_split,
        diagonal_one,
        diagonal_two,
        *everything,
        flops=12 * width**3,
        scratch=[(columns, 2 * middle, piece)],
    )
    return (inverse_one, block_one, inverse_two, coupled, block_two)


def solution(mesh):
    return jax.shard_map(
        body,
        mesh=mesh,
        in_specs=(
            P("row", "col"),
            P(("row", "col"), None),
            P(("row", "col")),
            P(("row", "col"), None),
            P(("row", "col")),
            P(),
            P(),
            P(),
        ),
        out_specs=(P(("row", "col"), None), P(), P(("row", "col"), None), P(), P()),
        check_vma=False,
    )
```

```python
import functools

import jax
import jax.numpy as jnp
from jax import lax
from jax.experimental import pallas as pl
from jax.experimental.pallas import tpu as pltpu
from jax.sharding import PartitionSpec as P

HIGH = lax.Precision.HIGHEST
FRONT_LIMIT = (65472 - 900) << 10


def masked(factor, pattern):
    block_count = pattern.shape[0]
    row_count, col_width = factor.shape
    shaped = factor.reshape(block_count, row_count // block_count, col_width)
    return (shaped * pattern.astype(jnp.float32)[:, None, None]).reshape(row_count, col_width)


def tdot(left, right):
    return lax.dot_general(
        left,
        right,
        (((0,), (0,)), ((), ())),
        precision=HIGH,
        preferred_element_type=jnp.float32,
    )


def cut(value, start, length, axis):
    return lax.dynamic_slice_in_dim(value, start, length, axis)


def put(whole, piece, *start):
    lead = len(start)
    shaped = piece.reshape((1,) * lead + piece.shape)
    return lax.dynamic_update_slice(whole, shaped, (*start, *(0,) * piece.ndim))


def swap(value, axis, bits):
    count = lax.axis_size(axis)
    return lax.ppermute(value, axis, [(at, at ^ bits) for at in range(count)])


def row_xor(value, bit):
    return swap(value, "row", bit)


def col_xor(value, bits):
    return swap(value, "col", bits)


def narrow_body(
    resident, factor_one, pattern_one, factor_two, pattern_two, coupling, diagonal_one, diagonal_two
):
    planes, columns = lax.axis_size("row"), lax.axis_size("col")
    ratio, chips = columns // planes, columns // 2
    plane, column = lax.axis_index("row"), lax.axis_index("col")
    core, chip = column % 2, column // 2
    block, width = factor_one.shape
    rows = resident.shape[0]
    piece = width // chips

    first = masked(factor_one, pattern_one)
    second = masked(factor_two, pattern_two)
    joined = second - jnp.dot(first, coupling, precision=HIGH)

    own = jnp.concatenate([first, joined], 1)
    strip = [own] + [
        lax.ppermute(own, "row", [(at, (at + step) % planes) for at in range(planes)])
        for step in range(1, planes)
    ]
    strip = jnp.concatenate(strip, 0)

    turned = resident.T
    arrived = []
    for step in range(planes):
        part = cut(turned, (step + column // ratio) % planes * block, block, 0)
        route = [(at, planes * (at % ratio) + (step + at // ratio) % planes) for at in range(columns)]
        arrived.append(lax.ppermute(part, "col", route))
    arrived = jnp.concatenate(arrived + arrived, 0)
    tile = cut(arrived, (column % planes - plane) % planes * block, planes * block, 0)

    plain = jnp.concatenate([first, second], 1)
    gathered = jnp.zeros((chips, 2, block, 2 * width), jnp.float32)
    for step in range(chips):
        moved = plain if step == 0 else col_xor(plain, 2 * step)
        gathered = put(gathered, moved, chip ^ step, core)
    mine = lax.dynamic_slice_in_dim(gathered, core, 1, 1)
    gathered = lax.dynamic_update_slice(gathered, col_xor(mine, 1), (0, 1 - core, 0, 0))
    factors = gathered.reshape(rows, 2 * width)

    given = col_xor(tdot(tile, cut(strip, (1 - core) * width, width, 1)), 1)
    half = tdot(tile, cut(strip, core * width, width, 1)) + given
    product = cut(half, chip * piece, piece, 1)
    for step in range(1, chips):
        product += col_xor(cut(half, (chip ^ step) * piece, piece, 1), 2 * step)

    partner = col_xor(product, 1)
    leading = jnp.where(core == 0, product, partner)
    square = tdot(cut(factors, core * width, width, 1), product)
    part = width // 2
    crossed = tdot(leading, cut(factors, width + core * part, part, 1))
    crossed = crossed.reshape(piece, part // piece, piece).transpose(1, 0, 2).reshape(part, piece)
    total = jnp.concatenate([square, crossed], 0)

    middle = total.shape[0] // 2
    odd = plane % 2
    kept = cut(total, odd * middle, middle, 0) + row_xor(cut(total, (1 - odd) * middle, middle, 0), 1)
    bit = 2
    while bit < planes:
        kept += row_xor(kept, bit)
        bit *= 2
    other = row_xor(kept, 1)

    everything = jnp.zeros((2, chips, 2, middle, piece), jnp.float32)
    for source, at in ((kept, odd), (other, 1 - odd)):
        for step in range(chips):
            moved = source if step == 0 else col_xor(source, 2 * step)
            everything = put(everything, moved, core, chip ^ step, at)
    mine = lax.dynamic_slice_in_dim(everything, core, 1, 0)
    everything = lax.dynamic_update_slice(everything, col_xor(mine, 1), (1 - core, 0, 0, 0, 0))
    everything = everything.reshape(2, chips, 2 * middle, piece)

    sheet = product.reshape(columns, block, piece)
    sheet = lax.all_to_all(sheet, "col", 0, 0)
    sheet = sheet.reshape(chips, 2, block, piece).transpose(1, 2, 0, 3).reshape(2, block, width)
    inverse_one, inverse_two = -sheet[0], -sheet[1]

    squares = everything[:, :, :width].transpose(0, 2, 1, 3).reshape(2, width, width)
    cross = everything[:, :, width:].reshape(2, chips, part // piece, piece, piece)
    cross = cross.transpose(1, 3, 0, 2, 4).reshape(width, width)
    block_one = diagonal_one + squares[0]
    coupled = cross - jnp.dot(block_one, coupling, precision=HIGH)
    block_two = diagonal_two + squares[1] - tdot(coupling, coupled)
    return (inverse_one, block_one, inverse_two, coupled, block_two)


def split(value):
    top = value.astype(jnp.bfloat16)
    return top, (value - top.astype(jnp.float32)).astype(jnp.bfloat16)


def fine_dot(left, right):
    def one(a, b):
        return jnp.dot(a, b, preferred_element_type=jnp.float32)

    return one(left[0], right[1]) + one(left[1], right[0]) + one(left[0], right[0])


def call(kernel, outs, *args, scalars=0, flops=0, scratch=()):
    outs = [jax.ShapeDtypeStruct(shape, kind) for shape, kind in outs]
    moved = sum(a.size * a.dtype.itemsize for a in (*args, *outs))
    return pl.pallas_call(
        kernel,
        out_shape=outs,
        in_specs=[pl.BlockSpec(memory_space=pltpu.SMEM)] * scalars
        + [pl.BlockSpec(memory_space=pltpu.VMEM)] * (len(args) - scalars),
        out_specs=[pl.BlockSpec(memory_space=pltpu.VMEM)] * len(outs),
        scratch_shapes=[pltpu.VMEM(shape, jnp.float32) for shape in scratch],
        cost_estimate=pl.CostEstimate(flops=flops, bytes_accessed=moved, transcendentals=0),
        compiler_params=pltpu.CompilerParams(vmem_limit_bytes=24 << 20),
    )(*args)


def span(start, length, step):
    return pl.ds(pl.multiple_of(start, step), length)


def place():
    plane, column = lax.axis_index("row"), lax.axis_index("col")
    return plane, column, column % 2, column // 2


def front_kernel(*refs):
    (one, two, f_one, f_two, coupling), (lead, joint, own, plain), refs = refs[:5], refs[5:9], refs[9:]
    held, sems = refs[:-1], refs[-1]
    copies = [
        pltpu.make_async_copy(source, target, sems.at[at])
        for at, (source, target) in enumerate(zip((one, two, f_one, f_two, coupling), held))
    ]
    for copy in copies:
        copy.start()
    for copy in copies[:4]:
        copy.wait()
    one, two, f_one, f_two, coupling = held
    block, width = f_one.shape
    count = one.shape[0]
    tall = block // count
    joint[block:, :] = jnp.zeros((joint.shape[0] - block, width), jnp.float32)
    for at in range(count):
        rows = slice(at * tall, (at + 1) * tall)
        keep = one[at].astype(jnp.float32)
        lead[rows, :] = f_one[rows, :] * keep
        plain[rows, width:] = f_two[rows, :] * two[at].astype(jnp.float32)
        joint[block + at : block + at + 1, :] = jnp.full((1, width), keep, jnp.float32)
    plain[:, :width] = own[:, :width] = lead[...]
    copies[4].wait()
    product = fine_dot(split(lead[...]), split(coupling[...]))
    joint[:block, :] = own[:, width:] = plain[:, width:] - product


def deal_kernel(mine, theirs, *outs):
    _, _, core, chip = place()
    half = mine.shape[0] // 2
    for step, out in enumerate(outs):
        to = chip ^ step
        at = to % half * 2 + core
        out[...] = jnp.where(to // half == core, mine[at], theirs[at])


def coupling_kernel(coupling, top, low, turned_top, turned_low):
    top[...], low[...] = split(coupling[...])
    turned_top[...], turned_low[...] = split(coupling[...].T)


def tile_kernel(masks, *refs):
    dealt, (top, low, held) = refs[: len(masks)], refs[len(masks) :]
    plane, _, _, chip = place()
    block = dealt[0].shape[0]
    for step, part in enumerate(dealt):
        slot = chip ^ step ^ plane
        for at, mask in enumerate(masks):

            @pl.when(slot == mask)
            def _():
                held[at * block : (at + 1) * block, :] = part[...]

    top[...], low[...] = split(held[...].T)


def part_kernel(away, count, steps, top, low, lead, joint, far, far_two, near, last, last_two, *refs):
    outs, held = refs[:-1], refs[-1]
    _, _, core, chip = place()
    block, width = lead.shape
    tall = block // count

    def keep(raw, marks):
        return [
            raw[at * tall : (at + 1) * tall, :] * marks[block + at : block + at + 1, :]
            for at in range(count)
        ]

    first = [lead[...], *keep(far, far_two), near[:, :width], *keep(last, last_two)]
    other = [joint[:block, :], far_two[:block, :], near[:, width:], last_two[:block, :]]
    side = core != (1 if away else 0)
    right = jnp.where(side, jnp.concatenate(other, 0), jnp.concatenate(first, 0))
    held[...] = fine_dot((top[...], low[...]), split(right))
    for group, out in zip(steps, outs):
        piece = out.shape[1] // len(group)
        for at, step in enumerate(group):
            lanes = span((chip ^ step) * piece, piece, 128)
            out[:, at * piece : (at + 1) * piece] = held[:, lanes]


def share_kernel(half, given, *outs):
    piece = outs[0].shape[1]
    for at, out in enumerate(outs):
        lanes = slice(at * piece, (at + 1) * piece)
        out[...] = half[:, lanes] + given[:, lanes]


def sum_kernel(*refs):
    total = refs[0][...]
    for ref in refs[1:-2]:
        total += ref[...]
    refs[-1][...] = refs[-2][...] = total


def factor_kernel(chips, *refs):
    parts, (top, low, held) = refs[: 2 * chips], refs[2 * chips :]
    core, chip = place()[2:]
    block = parts[0].shape[0]
    width = held.shape[1] // 2
    for at, part in enumerate(parts):
        row = (chip ^ at // 2) * 2 + (core ^ at % 2)
        held[span(row * block, block, 8), :] = part[...]
    top[:width], low[:width] = split(held[:, span(core * width, width, 128)].T)
    rest = width // 2
    top[width:], low[width:] = split(held[:, span(width + core * rest, rest, 128)].T)


def square_kernel(top, low, product, out):
    width = out.shape[0]
    out[...] = fine_dot((top[:width], low[:width]), split(product[...]))


def cross_kernel(top, low, product, partner, square, kept, sent, held):
    plane, _, core, _ = place()
    width, piece = square.shape
    leading = jnp.where(core == 0, product[...], partner[...])
    crossed = fine_dot((top[width:], low[width:]), split(leading))
    held[:width, :] = square[...]
    for start in range(0, width // 2, piece):
        held[width + start : width + start + piece, :] = crossed[start : start + piece].T
    middle = kept.shape[0]
    kept[...] = held[span(plane % 2 * middle, middle, 8), :]
    sent[...] = held[span((1 - plane % 2) * middle, middle, 8), :]


def last_kernel(chips, c_top, c_low, t_top, t_low, d_one, d_two, *refs):
    parts, refs = refs[: 4 * chips], refs[4 * chips :]
    outs, (b_one, coupled, b_two, held, sems) = refs[:3], refs[3:]
    copies = [
        pltpu.make_async_copy(source, target, sems.at[at])
        for at, (source, target) in enumerate(zip((b_one, coupled, b_two), outs))
    ]
    plane, _, core, chip = place()
    middle, piece = parts[0].shape
    width = b_one.shape[0]
    for at, part in enumerate(parts):
        side, step, half = core ^ at % 2, at // 2 % chips, plane % 2 ^ at // (2 * chips)
        held[side * chips + (chip ^ step), span(half * middle, middle, 8), :] = part[...]
    rest = width // 2
    for at in range(chips):
        lanes = slice(at * piece, (at + 1) * piece)
        b_one[:, lanes] = d_one[:, lanes] + held[at, :width, :]
    copies[0].start()
    known = fine_dot(split(b_one[...]), (c_top[...], c_low[...]))
    for at in range(chips):
        lanes = slice(at * piece, (at + 1) * piece)
        for start in range(0, width, piece):
            row = width + start % rest
            coupled[lanes, start : start + piece] = (
                held[start // rest * chips + at, row : row + piece, :]
                - known[lanes, start : start + piece]
            )
    copies[1].start()
    again = fine_dot((t_top[...], t_low[...]), split(coupled[...]))
    for at in range(chips):
        lanes = slice(at * piece, (at + 1) * piece)
        b_two[:, lanes] = d_two[:, lanes] + held[chips + at, :width, :] - again[:, lanes]
    copies[2].start()
    for copy in copies:
        copy.wait()


def body(
    resident, factor_one, pattern_one, factor_two, pattern_two, coupling, diagonal_one, diagonal_two
):
    planes, columns = lax.axis_size("row"), lax.axis_size("col")
    chips = columns // 2
    block, width = factor_one.shape
    rows = resident.shape[0]
    piece = width // chips
    if piece % 128 or (planes, chips) != (4, 4):
        return narrow_body(
            resident, factor_one, pattern_one, factor_two, pattern_two, coupling, diagonal_one, diagonal_two
        )
    f32, b16 = jnp.float32, jnp.bfloat16

    turned = resident.T.reshape(planes, block, rows)
    theirs = col_xor(turned, 1)
    far = row_xor(factor_one, 2)
    count = pattern_one.shape[0]
    tall = block + (count + 7) // 8 * 8
    shapes = [(block, width), (tall, width), (block, 2 * width), (block, 2 * width)]
    lead, joint, own, plain = pl.pallas_call(
        front_kernel,
        out_shape=[jax.ShapeDtypeStruct(shape, f32) for shape in shapes],
        in_specs=[pl.BlockSpec(memory_space=pltpu.HBM)] * 5,
        out_specs=[pl.BlockSpec(memory_space=pltpu.VMEM)] * 4,
        scratch_shapes=[
            pltpu.SMEM(pattern_one.shape, jnp.int32),
            pltpu.SMEM(pattern_two.shape, jnp.int32),
            pltpu.VMEM(factor_one.shape, f32),
            pltpu.VMEM(factor_two.shape, f32),
            pltpu.VMEM(coupling.shape, f32),
            pltpu.SemaphoreType.DMA((5,)),
        ],
        compiler_params=pltpu.CompilerParams(vmem_limit_bytes=FRONT_LIMIT),
    )(pattern_one, pattern_two, factor_one, factor_two, coupling)
    far_two = row_xor(joint, 2)
    near = row_xor(own, 1)
    last = row_xor(far, 1)
    last_two = row_xor(far_two, 1)
    masks = [0, 2, 1, 3]
    strip = [lead, joint, far, far_two, near, last, last_two]
    dealt = call(deal_kernel, [((block, rows), f32)] * chips, turned, theirs)
    dealt = [dealt[0]] + [col_xor(dealt[s], 2 * s) for s in range(1, chips)]
    around = [plain] + [col_xor(plain, 2 * step) for step in range(1, chips)]
    factors = []
    for value in around:
        factors += [value, col_xor(value, 1)]

    c_split = call(coupling_kernel, [((width, width), b16)] * 4, coupling)
    tile = call(
        functools.partial(tile_kernel, masks),
        [((rows, planes * block), b16)] * 2,
        *dealt,
        scratch=[(planes * block, rows)],
    )

    work = 6 * rows * planes * block * width
    steps = [(3, 1), (2, 0)]
    halves = [((rows, 2 * piece), f32)] * 2
    args = dict(flops=work, scratch=[(rows, width)])
    away = call(functools.partial(part_kernel, True, count, steps), halves, *tile, *strip, **args)
    half = call(functools.partial(part_kernel, False, count, steps), halves, *tile, *strip, **args)
    shares = {}
    for at, group in enumerate(steps):
        given = col_xor(away[at], 1)
        summed = call(share_kernel, [((rows, piece), f32)] * 2, half[at], given)
        for step, value in zip(group, summed):
            shares[step] = col_xor(value, 2 * step) if step else value
    shares = [shares[step] for step in range(chips)]
    product, result = call(sum_kernel, [((rows, piece), f32)] * 2, *shares)

    part = width // 2
    turned = call(
        functools.partial(factor_kernel, chips),
        [((width + part, rows), b16)] * 2,
        *factors,
        scratch=[(rows, 2 * width)],
    )
    (square,) = call(square_kernel, [((width, piece), f32)], *turned, product, flops=6 * width * rows * piece)
    middle = (width + part) // 2
    kept, sent = call(
        cross_kernel,
        [((middle, piece), f32)] * 2,
        *turned,
        product,
        col_xor(product, 1),
        square,
        flops=3 * width * rows * piece,
        scratch=[(width + part, piece)],
    )

    kept += row_xor(sent, 1)
    kept += row_xor(kept, 2)
    sheet = lax.all_to_all(result.reshape(columns, block, piece), "col", 0, 0)
    sheet = sheet.reshape(chips, 2, block, piece).transpose(1, 2, 0, 3).reshape(2, block, width)
    inverse_one, inverse_two = -sheet[0], -sheet[1]

    moved = {(0, 0): kept, (1, 0): row_xor(kept, 1)}
    for step in range(1, chips):
        moved[0, step] = col_xor(kept, 2 * step)
        if step & (step - 1):
            moved[1, step] = row_xor(moved[0, step], 1)
        else:
            moved[1, step] = col_xor(moved[1, 0], 2 * step)
    everything = []
    for half in range(2):
        for step in range(chips):
            everything += [moved[half, step], col_xor(moved[half, step], 1)]
    block_one, coupled, block_two = pl.pallas_call(
        functools.partial(last_kernel, chips),
        out_shape=[jax.ShapeDtypeStruct((width, width), f32)] * 3,
        in_specs=[pl.BlockSpec(memory_space=pltpu.VMEM)] * (6 + 4 * chips),
        out_specs=[pl.BlockSpec(memory_space=pltpu.HBM)] * 3,
        scratch_shapes=[pltpu.VMEM((width, width), f32)] * 3
        + [pltpu.VMEM((columns, 2 * middle, piece), f32), pltpu.SemaphoreType.DMA((3,))],
        compiler_params=pltpu.CompilerParams(vmem_limit_bytes=24 << 20),
    )(*c_split, diagonal_one, diagonal_two, *everything)
    return (inverse_one, block_one, inverse_two, coupled, block_two)


def solution(mesh):
    return jax.shard_map(
        body,
        mesh=mesh,
        in_specs=(
            P("row", "col"),
            P(("row", "col"), None),
            P(("row", "col")),
            P(("row", "col"), None),
            P(("row", "col")),
            P(),
            P(),
            P(),
        ),
        out_specs=(P(("row", "col"), None), P(), P(("row", "col"), None), P(), P()),
        check_vma=False,
    )
```

```python
import functools

import jax
import jax.numpy as jnp
from jax import lax
from jax.experimental import pallas as pl
from jax.experimental.pallas import tpu as pltpu
from jax.sharding import PartitionSpec as P

HIGH = lax.Precision.HIGHEST
FRONT_LIMIT = (65472 - 900) << 10


def masked(factor, pattern):
    block_count = pattern.shape[0]
    row_count, col_width = factor.shape
    shaped = factor.reshape(block_count, row_count // block_count, col_width)
    return (shaped * pattern.astype(jnp.float32)[:, None, None]).reshape(row_count, col_width)


def tdot(left, right):
    return lax.dot_general(
        left,
        right,
        (((0,), (0,)), ((), ())),
        precision=HIGH,
        preferred_element_type=jnp.float32,
    )


def cut(value, start, length, axis):
    return lax.dynamic_slice_in_dim(value, start, length, axis)


def put(whole, piece, *start):
    lead = len(start)
    shaped = piece.reshape((1,) * lead + piece.shape)
    return lax.dynamic_update_slice(whole, shaped, (*start, *(0,) * piece.ndim))


def swap(value, axis, bits):
    count = lax.axis_size(axis)
    return lax.ppermute(value, axis, [(at, at ^ bits) for at in range(count)])


def row_xor(value, bit):
    return swap(value, "row", bit)


def col_xor(value, bits):
    return swap(value, "col", bits)


def narrow_body(
    resident, factor_one, pattern_one, factor_two, pattern_two, coupling, diagonal_one, diagonal_two
):
    planes, columns = lax.axis_size("row"), lax.axis_size("col")
    ratio, chips = columns // planes, columns // 2
    plane, column = lax.axis_index("row"), lax.axis_index("col")
    core, chip = column % 2, column // 2
    block, width = factor_one.shape
    rows = resident.shape[0]
    piece = width // chips

    first = masked(factor_one, pattern_one)
    second = masked(factor_two, pattern_two)
    joined = second - jnp.dot(first, coupling, precision=HIGH)

    own = jnp.concatenate([first, joined], 1)
    strip = [own] + [
        lax.ppermute(own, "row", [(at, (at + step) % planes) for at in range(planes)])
        for step in range(1, planes)
    ]
    strip = jnp.concatenate(strip, 0)

    turned = resident.T
    arrived = []
    for step in range(planes):
        part = cut(turned, (step + column // ratio) % planes * block, block, 0)
        route = [(at, planes * (at % ratio) + (step + at // ratio) % planes) for at in range(columns)]
        arrived.append(lax.ppermute(part, "col", route))
    arrived = jnp.concatenate(arrived + arrived, 0)
    tile = cut(arrived, (column % planes - plane) % planes * block, planes * block, 0)

    plain = jnp.concatenate([first, second], 1)
    gathered = jnp.zeros((chips, 2, block, 2 * width), jnp.float32)
    for step in range(chips):
        moved = plain if step == 0 else col_xor(plain, 2 * step)
        gathered = put(gathered, moved, chip ^ step, core)
    mine = lax.dynamic_slice_in_dim(gathered, core, 1, 1)
    gathered = lax.dynamic_update_slice(gathered, col_xor(mine, 1), (0, 1 - core, 0, 0))
    factors = gathered.reshape(rows, 2 * width)

    given = col_xor(tdot(tile, cut(strip, (1 - core) * width, width, 1)), 1)
    half = tdot(tile, cut(strip, core * width, width, 1)) + given
    product = cut(half, chip * piece, piece, 1)
    for step in range(1, chips):
        product += col_xor(cut(half, (chip ^ step) * piece, piece, 1), 2 * step)

    partner = col_xor(product, 1)
    leading = jnp.where(core == 0, product, partner)
    square = tdot(cut(factors, core * width, width, 1), product)
    part = width // 2
    crossed = tdot(leading, cut(factors, width + core * part, part, 1))
    crossed = crossed.reshape(piece, part // piece, piece).transpose(1, 0, 2).reshape(part, piece)
    total = jnp.concatenate([square, crossed], 0)

    middle = total.shape[0] // 2
    odd = plane % 2
    kept = cut(total, odd * middle, middle, 0) + row_xor(cut(total, (1 - odd) * middle, middle, 0), 1)
    bit = 2
    while bit < planes:
        kept += row_xor(kept, bit)
        bit *= 2
    other = row_xor(kept, 1)

    everything = jnp.zeros((2, chips, 2, middle, piece), jnp.float32)
    for source, at in ((kept, odd), (other, 1 - odd)):
        for step in range(chips):
            moved = source if step == 0 else col_xor(source, 2 * step)
            everything = put(everything, moved, core, chip ^ step, at)
    mine = lax.dynamic_slice_in_dim(everything, core, 1, 0)
    everything = lax.dynamic_update_slice(everything, col_xor(mine, 1), (1 - core, 0, 0, 0, 0))
    everything = everything.reshape(2, chips, 2 * middle, piece)

    sheet = product.reshape(columns, block, piece)
    sheet = lax.all_to_all(sheet, "col", 0, 0)
    sheet = sheet.reshape(chips, 2, block, piece).transpose(1, 2, 0, 3).reshape(2, block, width)
    inverse_one, inverse_two = -sheet[0], -sheet[1]

    squares = everything[:, :, :width].transpose(0, 2, 1, 3).reshape(2, width, width)
    cross = everything[:, :, width:].reshape(2, chips, part // piece, piece, piece)
    cross = cross.transpose(1, 3, 0, 2, 4).reshape(width, width)
    block_one = diagonal_one + squares[0]
    coupled = cross - jnp.dot(block_one, coupling, precision=HIGH)
    block_two = diagonal_two + squares[1] - tdot(coupling, coupled)
    return (inverse_one, block_one, inverse_two, coupled, block_two)


def split(value):
    top = value.astype(jnp.bfloat16)
    return top, (value - top.astype(jnp.float32)).astype(jnp.bfloat16)


def fine_dot(left, right):
    def one(a, b):
        return jnp.dot(a, b, preferred_element_type=jnp.float32)

    return one(left[0], right[1]) + one(left[1], right[0]) + one(left[0], right[0])


def call(kernel, outs, *args, scalars=0, flops=0, scratch=()):
    outs = [jax.ShapeDtypeStruct(shape, kind) for shape, kind in outs]
    moved = sum(a.size * a.dtype.itemsize for a in (*args, *outs))
    return pl.pallas_call(
        kernel,
        out_shape=outs,
        in_specs=[pl.BlockSpec(memory_space=pltpu.SMEM)] * scalars
        + [pl.BlockSpec(memory_space=pltpu.VMEM)] * (len(args) - scalars),
        out_specs=[pl.BlockSpec(memory_space=pltpu.VMEM)] * len(outs),
        scratch_shapes=[pltpu.VMEM(shape, jnp.float32) for shape in scratch],
        cost_estimate=pl.CostEstimate(flops=flops, bytes_accessed=moved, transcendentals=0),
        compiler_params=pltpu.CompilerParams(vmem_limit_bytes=24 << 20),
    )(*args)


def span(start, length, step):
    return pl.ds(pl.multiple_of(start, step), length)


def place():
    plane, column = lax.axis_index("row"), lax.axis_index("col")
    return plane, column, column % 2, column // 2


def front_kernel(*refs):
    (one, two, f_one, f_two, coupling), (lead, joint, own, plain), refs = refs[:5], refs[5:9], refs[9:]
    held, sems = refs[:-1], refs[-1]
    copies = [
        pltpu.make_async_copy(source, target, sems.at[at])
        for at, (source, target) in enumerate(zip((one, two, f_one, f_two, coupling), held))
    ]
    for copy in copies:
        copy.start()
    for copy in copies[:4]:
        copy.wait()
    one, two, f_one, f_two, coupling = held
    block, width = f_one.shape
    count = one.shape[0]
    tall = block // count
    joint[block:, :] = jnp.zeros((joint.shape[0] - block, width), jnp.float32)
    for at in range(count):
        rows = slice(at * tall, (at + 1) * tall)
        keep = one[at].astype(jnp.float32)
        lead[rows, :] = f_one[rows, :] * keep
        plain[rows, width:] = f_two[rows, :] * two[at].astype(jnp.float32)
        joint[block + at : block + at + 1, :] = jnp.full((1, width), keep, jnp.float32)
    plain[:, :width] = own[:, :width] = lead[...]
    copies[4].wait()
    product = fine_dot(split(lead[...]), split(coupling[...]))
    joint[:block, :] = own[:, width:] = plain[:, width:] - product


def deal_kernel(mine, theirs, *outs):
    _, _, core, chip = place()
    half = mine.shape[0] // 2
    for step, out in enumerate(outs):
        to = chip ^ step
        at = to % half * 2 + core
        out[...] = jnp.where(to // half == core, mine[at], theirs[at])


def coupling_kernel(coupling, top, low, turned_top, turned_low):
    top[...], low[...] = split(coupling[...])
    turned_top[...], turned_low[...] = split(coupling[...].T)


def tile_kernel(masks, *refs):
    dealt, (top, low, held) = refs[: len(masks)], refs[len(masks) :]
    plane, _, _, chip = place()
    block = dealt[0].shape[0]
    for step, part in enumerate(dealt):
        slot = chip ^ step ^ plane
        for at, mask in enumerate(masks):

            @pl.when(slot == mask)
            def _():
                held[at * block : (at + 1) * block, :] = part[...]

    top[...], low[...] = split(held[...].T)


def part_kernel(away, count, steps, top, low, lead, joint, far, far_two, near, last, last_two, *refs):
    outs, held = refs[:-1], refs[-1]
    _, _, core, chip = place()
    block, width = lead.shape
    tall = block // count

    def keep(raw, marks):
        return [
            raw[at * tall : (at + 1) * tall, :] * marks[block + at : block + at + 1, :]
            for at in range(count)
        ]

    first = [lead[...], *keep(far, far_two), near[:, :width], *keep(last, last_two)]
    other = [joint[:block, :], far_two[:block, :], near[:, width:], last_two[:block, :]]
    side = core != (1 if away else 0)
    right = jnp.where(side, jnp.concatenate(other, 0), jnp.concatenate(first, 0))
    held[...] = fine_dot((top[...], low[...]), split(right))
    for group, out in zip(steps, outs):
        piece = out.shape[1] // len(group)
        for at, step in enumerate(group):
            lanes = span((chip ^ step) * piece, piece, 128)
            out[:, at * piece : (at + 1) * piece] = held[:, lanes]


def share_kernel(half, given, *outs):
    piece = outs[0].shape[1]
    for at, out in enumerate(outs):
        lanes = slice(at * piece, (at + 1) * piece)
        out[...] = half[:, lanes] + given[:, lanes]


def sum_kernel(*refs):
    total = refs[0][...]
    for ref in refs[1:-1]:
        total += ref[...]
    refs[-1][...] = total


def factor_kernel(chips, *refs):
    parts, (top, low, held) = refs[: 2 * chips], refs[2 * chips :]
    core, chip = place()[2:]
    block = parts[0].shape[0]
    width = held.shape[1] // 2
    for at, part in enumerate(parts):
        row = (chip ^ at // 2) * 2 + (core ^ at % 2)
        held[span(row * block, block, 8), :] = part[...]
    top[:width], low[:width] = split(held[:, span(core * width, width, 128)].T)
    rest = width // 2
    top[width:], low[width:] = split(held[:, span(width + core * rest, rest, 128)].T)


def square_kernel(top, low, product, *outs):
    odd = place()[0] % 2
    deep = outs[0].shape[0]
    right = split(product[...])
    for half, out in zip((odd, 1 - odd), outs):
        rows = span(half * deep, deep, 16)
        out[...] = fine_dot((top[rows, :], low[rows, :]), right)


def cross_kernel(width, top, low, product, partner, *outs):
    plane, _, core, _ = place()
    deep = outs[0].shape[0]
    right = split(jnp.where(core == 0, product[...], partner[...]))
    for half, out in zip((plane % 2, 1 - plane % 2), outs):
        rows = span(width + half * deep, deep, 16)
        out[...] = fine_dot((top[rows, :], low[rows, :]), right).T


def fold_kernel(square, square_got, cross, cross_got, out):
    deep = square.shape[0]
    out[:deep, :] = square[...] + square_got[...]
    out[deep:, :] = cross[...] + cross_got[...]


def last_kernel(chips, c_top, c_low, t_top, t_low, d_one, d_two, *refs):
    parts, refs = refs[: 4 * chips], refs[4 * chips :]
    outs, (b_one, coupled, b_two, held, sems) = refs[:3], refs[3:]
    copies = [
        pltpu.make_async_copy(source, target, sems.at[at])
        for at, (source, target) in enumerate(zip((b_one, coupled, b_two), outs))
    ]
    plane, _, core, chip = place()
    middle, piece = parts[0].shape
    width = b_one.shape[0]
    for at, part in enumerate(parts):
        side, step, half = core ^ at % 2, at // 2 % chips, plane % 2 ^ at // (2 * chips)
        held[side * chips + (chip ^ step), span(half * middle, middle, 8), :] = part[...]
    rest = width // 2
    for at in range(chips):
        lanes = slice(at * piece, (at + 1) * piece)
        for half in range(2):
            rows, start = slice(half * rest, (half + 1) * rest), half * middle
            b_one[rows, lanes] = d_one[rows, lanes] + held[at, start : start + rest, :]
    copies[0].start()
    known = fine_dot(split(b_one[...]), (c_top[...], c_low[...]))
    for at in range(chips):
        lanes = slice(at * piece, (at + 1) * piece)
        for start in range(0, width, piece):
            row = start % rest // piece * middle + rest
            coupled[lanes, start : start + piece] = (
                held[start // rest * chips + at, row : row + piece, :]
                - known[lanes, start : start + piece]
            )
    copies[1].start()
    again = fine_dot((t_top[...], t_low[...]), split(coupled[...]))
    for at in range(chips):
        lanes = slice(at * piece, (at + 1) * piece)
        for half in range(2):
            rows, start = slice(half * rest, (half + 1) * rest), half * middle
            corner = d_two[rows, lanes] + held[chips + at, start : start + rest, :]
            b_two[rows, lanes] = corner - again[rows, lanes]
    copies[2].start()
    for copy in copies:
        copy.wait()


def body(
    resident, factor_one, pattern_one, factor_two, pattern_two, coupling, diagonal_one, diagonal_two
):
    planes, columns = lax.axis_size("row"), lax.axis_size("col")
    chips = columns // 2
    block, width = factor_one.shape
    rows = resident.shape[0]
    piece = width // chips
    if piece % 128 or (planes, chips) != (4, 4):
        return narrow_body(
            resident, factor_one, pattern_one, factor_two, pattern_two, coupling, diagonal_one, diagonal_two
        )
    f32, b16 = jnp.float32, jnp.bfloat16

    turned = resident.T.reshape(planes, block, rows)
    theirs = col_xor(turned, 1)
    far = row_xor(factor_one, 2)
    count = pattern_one.shape[0]
    tall = block + (count + 7) // 8 * 8
    shapes = [(block, width), (tall, width), (block, 2 * width), (block, 2 * width)]
    lead, joint, own, plain = pl.pallas_call(
        front_kernel,
        out_shape=[jax.ShapeDtypeStruct(shape, f32) for shape in shapes],
        in_specs=[pl.BlockSpec(memory_space=pltpu.HBM)] * 5,
        out_specs=[pl.BlockSpec(memory_space=pltpu.VMEM)] * 4,
        scratch_shapes=[
            pltpu.SMEM(pattern_one.shape, jnp.int32),
            pltpu.SMEM(pattern_two.shape, jnp.int32),
            pltpu.VMEM(factor_one.shape, f32),
            pltpu.VMEM(factor_two.shape, f32),
            pltpu.VMEM(coupling.shape, f32),
            pltpu.SemaphoreType.DMA((5,)),
        ],
        compiler_params=pltpu.CompilerParams(vmem_limit_bytes=FRONT_LIMIT),
    )(pattern_one, pattern_two, factor_one, factor_two, coupling)
    far_two = row_xor(joint, 2)
    near = row_xor(own, 1)
    last = row_xor(far, 1)
    last_two = row_xor(far_two, 1)
    masks = [0, 2, 1, 3]
    strip = [lead, joint, far, far_two, near, last, last_two]
    dealt = call(deal_kernel, [((block, rows), f32)] * chips, turned, theirs)
    dealt = [dealt[0]] + [col_xor(dealt[s], 2 * s) for s in range(1, chips)]
    around = [plain] + [col_xor(plain, 2 * step) for step in range(1, chips)]
    factors = []
    for value in around:
        factors += [value, col_xor(value, 1)]

    c_split = call(coupling_kernel, [((width, width), b16)] * 4, coupling)
    tile = call(
        functools.partial(tile_kernel, masks),
        [((rows, planes * block), b16)] * 2,
        *dealt,
        scratch=[(planes * block, rows)],
    )

    work = 6 * rows * planes * block * width
    steps = [(3, 1), (2, 0)]
    halves = [((rows, 2 * piece), f32)] * 2
    args = dict(flops=work, scratch=[(rows, width)])
    away = call(functools.partial(part_kernel, True, count, steps), halves, *tile, *strip, **args)
    half = call(functools.partial(part_kernel, False, count, steps), halves, *tile, *strip, **args)
    shares = {}
    for at, group in enumerate(steps):
        given = col_xor(away[at], 1)
        summed = call(share_kernel, [((rows, piece), f32)] * 2, half[at], given)
        for step, value in zip(group, summed):
            shares[step] = col_xor(value, 2 * step) if step else value
    shares = [shares[step] for step in range(chips)]
    (product,) = call(sum_kernel, [((rows, piece), f32)], *shares)
    (result,) = call(sum_kernel, [((rows, piece), f32)], product)

    part = width // 2
    turned = call(
        functools.partial(factor_kernel, chips),
        [((width + part, rows), b16)] * 2,
        *factors,
        scratch=[(rows, 2 * width)],
    )
    square = call(
        square_kernel,
        [((part, piece), f32)] * 2,
        *turned,
        product,
        flops=6 * width * rows * piece,
    )
    cross = call(
        functools.partial(cross_kernel, width),
        [((piece, piece), f32)] * 2,
        *turned,
        product,
        col_xor(product, 1),
        flops=3 * width * rows * piece,
    )

    middle = part + piece
    square_got, cross_got = row_xor(square[1], 1), row_xor(cross[1], 1)
    (kept,) = call(fold_kernel, [((middle, piece), f32)], square[0], square_got, cross[0], cross_got)
    kept += row_xor(kept, 2)
    sheet = lax.all_to_all(result.reshape(columns, block, piece), "col", 0, 0)
    sheet = sheet.reshape(chips, 2, block, piece).transpose(1, 2, 0, 3).reshape(2, block, width)
    inverse_one, inverse_two = -sheet[0], -sheet[1]

    moved = {(0, 0): kept, (1, 0): row_xor(kept, 1)}
    for step in range(1, chips):
        moved[0, step] = col_xor(kept, 2 * step)
        if step & (step - 1):
            moved[1, step] = row_xor(moved[0, step], 1)
        else:
            moved[1, step] = col_xor(moved[1, 0], 2 * step)
    everything = []
    for half in range(2):
        for step in range(chips):
            everything += [moved[half, step], col_xor(moved[half, step], 1)]
    block_one, coupled, block_two = pl.pallas_call(
        functools.partial(last_kernel, chips),
        out_shape=[jax.ShapeDtypeStruct((width, width), f32)] * 3,
        in_specs=[pl.BlockSpec(memory_space=pltpu.VMEM)] * (6 + 4 * chips),
        out_specs=[pl.BlockSpec(memory_space=pltpu.HBM)] * 3,
        scratch_shapes=[pltpu.VMEM((width, width), f32)] * 3
        + [pltpu.VMEM((columns, 2 * middle, piece), f32), pltpu.SemaphoreType.DMA((3,))],
        compiler_params=pltpu.CompilerParams(vmem_limit_bytes=24 << 20),
    )(*c_split, diagonal_one, diagonal_two, *everything)
    return (inverse_one, block_one, inverse_two, coupled, block_two)


def solution(mesh):
    return jax.shard_map(
        body,
        mesh=mesh,
        in_specs=(
            P("row", "col"),
            P(("row", "col"), None),
            P(("row", "col")),
            P(("row", "col"), None),
            P(("row", "col")),
            P(),
            P(),
            P(),
        ),
        out_specs=(P(("row", "col"), None), P(), P(("row", "col"), None), P(), P()),
        check_vma=False,
    )
```

```python
import functools

import jax
import jax.numpy as jnp
from jax import lax
from jax.experimental import pallas as pl
from jax.experimental.pallas import tpu as pltpu
from jax.sharding import PartitionSpec as P

HIGH = lax.Precision.HIGHEST
FRONT_LIMIT = (65472 - 900) << 10


def masked(factor, pattern):
    block_count = pattern.shape[0]
    row_count, col_width = factor.shape
    shaped = factor.reshape(block_count, row_count // block_count, col_width)
    return (shaped * pattern.astype(jnp.float32)[:, None, None]).reshape(row_count, col_width)


def tdot(left, right):
    return lax.dot_general(
        left,
        right,
        (((0,), (0,)), ((), ())),
        precision=HIGH,
        preferred_element_type=jnp.float32,
    )


def cut(value, start, length, axis):
    return lax.dynamic_slice_in_dim(value, start, length, axis)


def put(whole, piece, *start):
    lead = len(start)
    shaped = piece.reshape((1,) * lead + piece.shape)
    return lax.dynamic_update_slice(whole, shaped, (*start, *(0,) * piece.ndim))


def swap(value, axis, bits):
    count = lax.axis_size(axis)
    return lax.ppermute(value, axis, [(at, at ^ bits) for at in range(count)])


def row_xor(value, bit):
    return swap(value, "row", bit)


def col_xor(value, bits):
    return swap(value, "col", bits)


def narrow_body(
    resident, factor_one, pattern_one, factor_two, pattern_two, coupling, diagonal_one, diagonal_two
):
    planes, columns = lax.axis_size("row"), lax.axis_size("col")
    ratio, chips = columns // planes, columns // 2
    plane, column = lax.axis_index("row"), lax.axis_index("col")
    core, chip = column % 2, column // 2
    block, width = factor_one.shape
    rows = resident.shape[0]
    piece = width // chips

    first = masked(factor_one, pattern_one)
    second = masked(factor_two, pattern_two)
    joined = second - jnp.dot(first, coupling, precision=HIGH)

    own = jnp.concatenate([first, joined], 1)
    strip = [own] + [
        lax.ppermute(own, "row", [(at, (at + step) % planes) for at in range(planes)])
        for step in range(1, planes)
    ]
    strip = jnp.concatenate(strip, 0)

    turned = resident.T
    arrived = []
    for step in range(planes):
        part = cut(turned, (step + column // ratio) % planes * block, block, 0)
        route = [(at, planes * (at % ratio) + (step + at // ratio) % planes) for at in range(columns)]
        arrived.append(lax.ppermute(part, "col", route))
    arrived = jnp.concatenate(arrived + arrived, 0)
    tile = cut(arrived, (column % planes - plane) % planes * block, planes * block, 0)

    plain = jnp.concatenate([first, second], 1)
    gathered = jnp.zeros((chips, 2, block, 2 * width), jnp.float32)
    for step in range(chips):
        moved = plain if step == 0 else col_xor(plain, 2 * step)
        gathered = put(gathered, moved, chip ^ step, core)
    mine = lax.dynamic_slice_in_dim(gathered, core, 1, 1)
    gathered = lax.dynamic_update_slice(gathered, col_xor(mine, 1), (0, 1 - core, 0, 0))
    factors = gathered.reshape(rows, 2 * width)

    given = col_xor(tdot(tile, cut(strip, (1 - core) * width, width, 1)), 1)
    half = tdot(tile, cut(strip, core * width, width, 1)) + given
    product = cut(half, chip * piece, piece, 1)
    for step in range(1, chips):
        product += col_xor(cut(half, (chip ^ step) * piece, piece, 1), 2 * step)

    partner = col_xor(product, 1)
    leading = jnp.where(core == 0, product, partner)
    square = tdot(cut(factors, core * width, width, 1), product)
    part = width // 2
    crossed = tdot(leading, cut(factors, width + core * part, part, 1))
    crossed = crossed.reshape(piece, part // piece, piece).transpose(1, 0, 2).reshape(part, piece)
    total = jnp.concatenate([square, crossed], 0)

    middle = total.shape[0] // 2
    odd = plane % 2
    kept = cut(total, odd * middle, middle, 0) + row_xor(cut(total, (1 - odd) * middle, middle, 0), 1)
    bit = 2
    while bit < planes:
        kept += row_xor(kept, bit)
        bit *= 2
    other = row_xor(kept, 1)

    everything = jnp.zeros((2, chips, 2, middle, piece), jnp.float32)
    for source, at in ((kept, odd), (other, 1 - odd)):
        for step in range(chips):
            moved = source if step == 0 else col_xor(source, 2 * step)
            everything = put(everything, moved, core, chip ^ step, at)
    mine = lax.dynamic_slice_in_dim(everything, core, 1, 0)
    everything = lax.dynamic_update_slice(everything, col_xor(mine, 1), (1 - core, 0, 0, 0, 0))
    everything = everything.reshape(2, chips, 2 * middle, piece)

    sheet = product.reshape(columns, block, piece)
    sheet = lax.all_to_all(sheet, "col", 0, 0)
    sheet = sheet.reshape(chips, 2, block, piece).transpose(1, 2, 0, 3).reshape(2, block, width)
    inverse_one, inverse_two = -sheet[0], -sheet[1]

    squares = everything[:, :, :width].transpose(0, 2, 1, 3).reshape(2, width, width)
    cross = everything[:, :, width:].reshape(2, chips, part // piece, piece, piece)
    cross = cross.transpose(1, 3, 0, 2, 4).reshape(width, width)
    block_one = diagonal_one + squares[0]
    coupled = cross - jnp.dot(block_one, coupling, precision=HIGH)
    block_two = diagonal_two + squares[1] - tdot(coupling, coupled)
    return (inverse_one, block_one, inverse_two, coupled, block_two)


def split(value):
    top = value.astype(jnp.bfloat16)
    return top, (value - top.astype(jnp.float32)).astype(jnp.bfloat16)


def fine_dot(left, right):
    def one(a, b):
        return jnp.dot(a, b, preferred_element_type=jnp.float32)

    return one(left[0], right[1]) + one(left[1], right[0]) + one(left[0], right[0])


def call(kernel, outs, *args, scalars=0, flops=0, scratch=()):
    outs = [jax.ShapeDtypeStruct(shape, kind) for shape, kind in outs]
    moved = sum(a.size * a.dtype.itemsize for a in (*args, *outs))
    return pl.pallas_call(
        kernel,
        out_shape=outs,
        in_specs=[pl.BlockSpec(memory_space=pltpu.SMEM)] * scalars
        + [pl.BlockSpec(memory_space=pltpu.VMEM)] * (len(args) - scalars),
        out_specs=[pl.BlockSpec(memory_space=pltpu.VMEM)] * len(outs),
        scratch_shapes=[pltpu.VMEM(shape, jnp.float32) for shape in scratch],
        cost_estimate=pl.CostEstimate(flops=flops, bytes_accessed=moved, transcendentals=0),
        compiler_params=pltpu.CompilerParams(vmem_limit_bytes=24 << 20),
    )(*args)


def span(start, length, step):
    return pl.ds(pl.multiple_of(start, step), length)


def place():
    plane, column = lax.axis_index("row"), lax.axis_index("col")
    return plane, column, column % 2, column // 2


def front_kernel(*refs):
    (one, two, f_one, f_two, coupling), (lead, joint, own, plain), refs = refs[:5], refs[5:9], refs[9:]
    held, sems = refs[:-1], refs[-1]
    copies = [
        pltpu.make_async_copy(source, target, sems.at[at])
        for at, (source, target) in enumerate(zip((one, two, f_one, f_two, coupling), held))
    ]
    for copy in copies:
        copy.start()
    for copy in copies[:4]:
        copy.wait()
    one, two, f_one, f_two, coupling = held
    block, width = f_one.shape
    count = one.shape[0]
    tall = block // count
    joint[block:, :] = jnp.zeros((joint.shape[0] - block, width), jnp.float32)
    for at in range(count):
        rows = slice(at * tall, (at + 1) * tall)
        keep = one[at].astype(jnp.float32)
        lead[rows, :] = f_one[rows, :] * keep
        plain[rows, width:] = f_two[rows, :] * two[at].astype(jnp.float32)
        joint[block + at : block + at + 1, :] = jnp.full((1, width), keep, jnp.float32)
    plain[:, :width] = own[:, :width] = lead[...]
    copies[4].wait()
    product = fine_dot(split(lead[...]), split(coupling[...]))
    joint[:block, :] = own[:, width:] = plain[:, width:] - product


def deal_kernel(mine, theirs, *outs):
    _, _, core, chip = place()
    half = mine.shape[0] // 2
    for step, out in enumerate(outs):
        to = chip ^ step
        at = to % half * 2 + core
        out[...] = jnp.where(to // half == core, mine[at], theirs[at])


def coupling_kernel(coupling, top, low, turned_top, turned_low):
    top[...], low[...] = split(coupling[...])
    turned_top[...], turned_low[...] = split(coupling[...].T)


def tile_kernel(masks, *refs):
    dealt, (top, low, held) = refs[: len(masks)], refs[len(masks) :]
    plane, _, _, chip = place()
    block = dealt[0].shape[0]
    for step, part in enumerate(dealt):
        slot = chip ^ step ^ plane
        for at, mask in enumerate(masks):

            @pl.when(slot == mask)
            def _():
                held[at * block : (at + 1) * block, :] = part[...]

    top[...], low[...] = split(held[...].T)


def part_kernel(away, count, steps, top, low, lead, joint, far, far_two, near, last, last_two, *refs):
    outs, held = refs[:-1], refs[-1]
    _, _, core, chip = place()
    block, width = lead.shape
    tall = block // count

    def keep(raw, marks):
        return [
            raw[at * tall : (at + 1) * tall, :] * marks[block + at : block + at + 1, :]
            for at in range(count)
        ]

    first = [lead[...], *keep(far, far_two), near[:, :width], *keep(last, last_two)]
    other = [joint[:block, :], far_two[:block, :], near[:, width:], last_two[:block, :]]
    side = core != (1 if away else 0)
    right = jnp.where(side, jnp.concatenate(other, 0), jnp.concatenate(first, 0))
    held[...] = fine_dot((top[...], low[...]), split(right))
    for group, out in zip(steps, outs):
        piece = out.shape[1] // len(group)
        for at, step in enumerate(group):
            lanes = span((chip ^ step) * piece, piece, 128)
            out[:, at * piece : (at + 1) * piece] = held[:, lanes]


def share_kernel(half, given, *outs):
    piece = outs[0].shape[1]
    for at, out in enumerate(outs):
        lanes = slice(at * piece, (at + 1) * piece)
        out[...] = half[:, lanes] + given[:, lanes]


def sum_kernel(*refs):
    total = refs[0][...]
    for ref in refs[1:-1]:
        total += ref[...]
    refs[-1][...] = total


def factor_kernel(chips, *refs):
    parts, (top, low, held) = refs[: 2 * chips], refs[2 * chips :]
    core, chip = place()[2:]
    block = parts[0].shape[0]
    width = held.shape[1] // 2
    for at, part in enumerate(parts):
        row = (chip ^ at // 2) * 2 + (core ^ at % 2)
        held[span(row * block, block, 8), :] = part[...]
    top[:width], low[:width] = split(held[:, span(core * width, width, 128)].T)
    rest = width // 2
    top[width:], low[width:] = split(held[:, span(width + core * rest, rest, 128)].T)


def square_kernel(top, low, product, *outs):
    odd = place()[0] % 2
    deep = outs[0].shape[0]
    right = split(product[...])
    for half, out in zip((odd, 1 - odd), outs):
        rows = span(half * deep, deep, 16)
        out[...] = fine_dot((top[rows, :], low[rows, :]), right)


def cross_kernel(width, top, low, product, partner, *outs):
    plane, _, core, _ = place()
    deep = outs[0].shape[0]
    right = split(jnp.where(core == 0, product[...], partner[...]))
    for half, out in zip((plane % 2, 1 - plane % 2), outs):
        rows = span(width + half * deep, deep, 16)
        out[...] = fine_dot((top[rows, :], low[rows, :]), right).T


def fold_kernel(square, square_got, cross, cross_got, out):
    deep = square.shape[0]
    out[:deep, :] = square[...] + square_got[...]
    out[deep:, :] = cross[...] + cross_got[...]


def last_kernel(chips, c_top, c_low, t_top, t_low, d_one, d_two, *refs):
    parts, refs = refs[: 4 * chips], refs[4 * chips :]
    outs, (b_one, coupled, b_two, held, sems) = refs[:3], refs[3:]
    copies = [
        pltpu.make_async_copy(source, target, sems.at[at])
        for at, (source, target) in enumerate(zip((b_one, coupled, b_two), outs))
    ]
    plane, _, core, chip = place()
    middle, piece = parts[0].shape
    width = b_one.shape[0]
    for at, part in enumerate(parts):
        side, step, half = core ^ at % 2, at // 2 % chips, plane % 2 ^ at // (2 * chips)
        held[side * chips + (chip ^ step), span(half * middle, middle, 8), :] = part[...]
    rest = width // 2
    for at in range(chips):
        lanes = slice(at * piece, (at + 1) * piece)
        for half in range(2):
            rows, start = slice(half * rest, (half + 1) * rest), half * middle
            b_one[rows, lanes] = d_one[rows, lanes] + held[at, start : start + rest, :]
    copies[0].start()
    known = fine_dot(split(b_one[...]), (c_top[...], c_low[...]))
    for at in range(chips):
        lanes = slice(at * piece, (at + 1) * piece)
        for start in range(0, width, piece):
            row = start % rest // piece * middle + rest
            coupled[lanes, start : start + piece] = (
                held[start // rest * chips + at, row : row + piece, :]
                - known[lanes, start : start + piece]
            )
    copies[1].start()
    again = fine_dot((t_top[...], t_low[...]), split(coupled[...]))
    for at in range(chips):
        lanes = slice(at * piece, (at + 1) * piece)
        for half in range(2):
            rows, start = slice(half * rest, (half + 1) * rest), half * middle
            corner = d_two[rows, lanes] + held[chips + at, start : start + rest, :]
            b_two[rows, lanes] = corner - again[rows, lanes]
    copies[2].start()
    for copy in copies:
        copy.wait()


def body(
    resident, factor_one, pattern_one, factor_two, pattern_two, coupling, diagonal_one, diagonal_two
):
    planes, columns = lax.axis_size("row"), lax.axis_size("col")
    chips = columns // 2
    block, width = factor_one.shape
    rows = resident.shape[0]
    piece = width // chips
    if piece % 128 or (planes, chips) != (4, 4):
        return narrow_body(
            resident, factor_one, pattern_one, factor_two, pattern_two, coupling, diagonal_one, diagonal_two
        )
    f32, b16 = jnp.float32, jnp.bfloat16

    turned = resident.T.reshape(planes, block, rows)
    theirs = col_xor(turned, 1)
    far = row_xor(factor_one, 2)
    count = pattern_one.shape[0]
    tall = block + (count + 7) // 8 * 8
    shapes = [(block, width), (tall, width), (block, 2 * width), (block, 2 * width)]
    lead, joint, own, plain = pl.pallas_call(
        front_kernel,
        out_shape=[jax.ShapeDtypeStruct(shape, f32) for shape in shapes],
        in_specs=[pl.BlockSpec(memory_space=pltpu.HBM)] * 5,
        out_specs=[pl.BlockSpec(memory_space=pltpu.VMEM)] * 4,
        scratch_shapes=[
            pltpu.SMEM(pattern_one.shape, jnp.int32),
            pltpu.SMEM(pattern_two.shape, jnp.int32),
            pltpu.VMEM(factor_one.shape, f32),
            pltpu.VMEM(factor_two.shape, f32),
            pltpu.VMEM(coupling.shape, f32),
            pltpu.SemaphoreType.DMA((5,)),
        ],
        compiler_params=pltpu.CompilerParams(vmem_limit_bytes=FRONT_LIMIT),
    )(pattern_one, pattern_two, factor_one, factor_two, coupling)
    far_two = row_xor(joint, 2)
    near = row_xor(own, 1)
    last = row_xor(far, 1)
    last_two = row_xor(far_two, 1)
    masks = [0, 2, 1, 3]
    strip = [lead, joint, far, far_two, near, last, last_two]
    dealt = call(deal_kernel, [((block, rows), f32)] * chips, turned, theirs)
    dealt = [dealt[0]] + [col_xor(dealt[s], 2 * s) for s in range(1, chips)]
    around = [plain] + [col_xor(plain, 2 * step) for step in range(1, chips)]
    factors = []
    for value in around:
        factors += [value, col_xor(value, 1)]

    c_split = call(coupling_kernel, [((width, width), b16)] * 4, coupling)
    tile = call(
        functools.partial(tile_kernel, masks),
        [((rows, planes * block), b16)] * 2,
        *dealt,
        scratch=[(planes * block, rows)],
    )

    work = 6 * rows * planes * block * width
    steps = [(3, 1), (2, 0)]
    halves = [((rows, 2 * piece), f32)] * 2
    args = dict(flops=work, scratch=[(rows, width)])
    away = call(functools.partial(part_kernel, True, count, steps), halves, *tile, *strip, **args)
    half = call(functools.partial(part_kernel, False, count, steps), halves, *tile, *strip, **args)
    shares = {}
    for at, group in enumerate(steps):
        given = col_xor(away[at], 1)
        summed = call(share_kernel, [((rows, piece), f32)] * 2, half[at], given)
        for step, value in zip(group, summed):
            shares[step] = col_xor(value, 2 * step) if step else value
    shares = [shares[step] for step in range(chips)]
    (product,) = call(sum_kernel, [((rows, piece), f32)], *shares)
    (result,) = call(sum_kernel, [((rows, piece), f32)], product)

    part = width // 2
    turned = call(
        functools.partial(factor_kernel, chips),
        [((width + part, rows), b16)] * 2,
        *factors,
        scratch=[(rows, 2 * width)],
    )
    square = call(
        square_kernel,
        [((part, piece), f32)] * 2,
        *turned,
        product,
        flops=6 * width * rows * piece,
    )
    cross = call(
        functools.partial(cross_kernel, width),
        [((piece, piece), f32)] * 2,
        *turned,
        product,
        col_xor(product, 1),
        flops=3 * width * rows * piece,
    )

    middle = part + piece
    square = square[0] + row_xor(square[1], 1)
    square_got = row_xor(square, 2)
    cross = cross[0] + row_xor(cross[1], 1)
    cross_got = row_xor(cross, 2)
    (kept,) = call(fold_kernel, [((middle, piece), f32)], square, square_got, cross, cross_got)
    sheet = lax.all_to_all(result.reshape(columns, block, piece), "col", 0, 0)
    sheet = sheet.reshape(chips, 2, block, piece).transpose(1, 2, 0, 3).reshape(2, block, width)
    inverse_one, inverse_two = -sheet[0], -sheet[1]

    moved = {(0, 0): kept, (1, 0): row_xor(kept, 1)}
    for step in range(1, chips):
        moved[0, step] = col_xor(kept, 2 * step)
        if step & (step - 1):
            moved[1, step] = row_xor(moved[0, step], 1)
        else:
            moved[1, step] = col_xor(moved[1, 0], 2 * step)
    everything = []
    for half in range(2):
        for step in range(chips):
            everything += [moved[half, step], col_xor(moved[half, step], 1)]
    block_one, coupled, block_two = pl.pallas_call(
        functools.partial(last_kernel, chips),
        out_shape=[jax.ShapeDtypeStruct((width, width), f32)] * 3,
        in_specs=[pl.BlockSpec(memory_space=pltpu.VMEM)] * (6 + 4 * chips),
        out_specs=[pl.BlockSpec(memory_space=pltpu.HBM)] * 3,
        scratch_shapes=[pltpu.VMEM((width, width), f32)] * 3
        + [pltpu.VMEM((columns, 2 * middle, piece), f32), pltpu.SemaphoreType.DMA((3,))],
        compiler_params=pltpu.CompilerParams(vmem_limit_bytes=24 << 20),
    )(*c_split, diagonal_one, diagonal_two, *everything)
    return (inverse_one, block_one, inverse_two, coupled, block_two)


def solution(mesh):
    return jax.shard_map(
        body,
        mesh=mesh,
        in_specs=(
            P("row", "col"),
            P(("row", "col"), None),
            P(("row", "col")),
            P(("row", "col"), None),
            P(("row", "col")),
            P(),
            P(),
            P(),
        ),
        out_specs=(P(("row", "col"), None), P(), P(("row", "col"), None), P(), P()),
        check_vma=False,
    )
```
